32 devices in a mesh: dp: 16 (over z, y, x), mp: 2 (over core).
Axes of the slice: x: 2, y: 2, z: 4, core: 2. Of those that a mesh axis runs over, the one named last changes fastest.
Arguments:
- tokens: bfloat16 [24576, 768], P('dp', 'mp'), may hold values from -6 to 6
- norm1_gain: float32 [768], replicated, may hold values from 0.5 to 1.5
- norm1_bias: float32 [768], replicated, may hold values from -1.5 to 1.5
- qkv_weight: bfloat16 [768, 3, 768], P(None, None, 'mp'), may hold values from -0.21875 to 0.21875
- qv_bias: float32 [2, 768], P(None, 'mp'), may hold values from -2.5 to 2.5
- out_weight: bfloat16 [768, 768], P('mp'), may hold values from -2 to 2
- out_bias: float32 [768], replicated, may hold values from -1.5 to 1.5
- norm2_gain: float32 [768], replicated, may hold values from 0.5 to 1.5
- norm2_bias: float32 [768], replicated, may hold values from -1.5 to 1.5
- up_weight: bfloat16 [768, 3072], P(None, 'mp'), may hold values from -0.21875 to 0.21875
- up_bias: float32 [3072], P('mp'), may hold values from -2.5 to 2.5
- down_weight: bfloat16 [3072, 768], P('mp'), may hold values from -0.109375 to 0.109375
- down_bias: float32 [768], replicated, may hold values from -1.5 to 1.5
- out_grad: bfloat16 [24576, 768], P('dp', 'mp'), may hold values from -6 to 6
- send_slot: int32 [24576], P('dp'), may hold values from 0 to 3071, as said below
- pack_index: int32 [24576], P('dp'), may hold values from 0 to 3071, as said below
- clip_ids: int32 [24576], P('dp'), may hold values from 0 to 3, as said below
Outputs:
- out: bfloat16 [24576, 768], P('dp', 'mp')
- tokens_grad: bfloat16 [24576, 768], P('dp', 'mp')
- norm1_gain_grad: float32 [768], replicated
- norm1_bias_grad: float32 [768], replicated
- qkv_weight_grad: float32 [768, 3, 768], P('dp', None, 'mp')
- qv_bias_grad: float32 [2, 768], P(None, 'mp')
- out_weight_grad: float32 [768, 768], P('mp', 'dp')
- out_bias_grad: float32 [768], replicated
- norm2_gain_grad: float32 [768], replicated
- norm2_bias_grad: float32 [768], replicated
- up_weight_grad: float32 [768, 3072], P('dp', 'mp')
- up_bias_grad: float32 [3072], P('mp')
- down_weight_grad: float32 [3072, 768], P('mp', 'dp')
- down_bias_grad: float32 [768], replicated
The draws below stay inside these ranges and needn't reach their ends.
Inputs may be any that keep to these rules, and one draw needn't show every extreme that they name: `send_slot`: on each index of dp the 1536 rows name distinct slots; slot // 192 is the group that receives the row. Each index sends exactly 192 rows to half of the groups and none to the others, and each group receives from exactly half of the indices. `pack_index`: arriving slot s = i * 192 + j of a group holds the row that index i of dp sent with slot (group * 192 + j); the 1536 packed rows of a group name distinct slots that all carry a row. `clip_ids`: never falling along a group's packed rows; rows attend only to rows of their group with the same number. Some group holds a clip of exactly 1190 rows.
All inputs are finite; a program needn't handle non-finite values.
Results may differ from the reference program's by a relative error of at most 0.018.
Values may be sent and summed in bfloat16 or wider, within the bound.
No kernel may reach another device: no remote copies, remote signals or barrier semaphores. Data moves between devices by JAX's collectives and lax.ppermute only.
A program may use at most 256 MiB of HBM per device.

```python
import jax
import jax.numpy as jnp
from jax import lax

D = 768
HEADS = 12
HEAD_DIM = 64
FF = 3072
TOK_DEV = 1536
FULL_LEN = 1190
GROUPS = 16
CAP = 192
TOKENS = 24576


def route_plan(key):
    row_key, col_key = jax.random.split(jax.random.fold_in(key, 7))
    sender_order = jax.random.permutation(row_key, GROUPS)
    group_order = jax.random.permutation(col_key, GROUPS)
    return (sender_order[:, None] + group_order[None, :]) % 2 == 0


def pick_slots(flags, sub_key):
    score = jnp.where(flags, 0, GROUPS).astype(jnp.int32) + jnp.arange(GROUPS, dtype=jnp.int32)
    chosen = jnp.argsort(score)[:GROUPS // 2].astype(jnp.int32)
    slots = (chosen[:, None] * CAP + jnp.arange(CAP, dtype=jnp.int32)[None, :]).reshape(-1)
    return jax.random.permutation(sub_key, slots)


def draw_send_slot(key, part):
    linked = route_plan(key)
    sub_keys = jax.random.split(jax.random.fold_in(key, 11), GROUPS)
    return jax.vmap(pick_slots)(linked, sub_keys).reshape(-1).astype(jnp.int32)


def draw_pack_index(key, part):
    linked = route_plan(key)
    sub_keys = jax.random.split(jax.random.fold_in(key, 13), GROUPS)
    return jax.vmap(pick_slots)(linked.T, sub_keys).reshape(-1).astype(jnp.int32)


def draw_clip_ids(key, part):
    full_key, first_key, second_key = jax.random.split(jax.random.fold_in(key, 17), 3)
    whole = (jax.random.randint(full_key, (GROUPS,), 0, 2) == 1) | (jnp.arange(GROUPS) == 0)
    half_rows = TOK_DEV // 2
    least = TOK_DEV // 5
    first_cut = jax.random.randint(first_key, (GROUPS,), least, half_rows - least + 1)
    second_cut = jax.random.randint(second_key, (GROUPS,), least, half_rows - least + 1)
    position = jnp.arange(TOK_DEV, dtype=jnp.int32)[None, :]
    split_ids = (position >= first_cut[:, None]).astype(jnp.int32) + (position >= half_rows).astype(jnp.int32) + (position >= half_rows + second_cut[:, None]).astype(jnp.int32)
    full_ids = jnp.broadcast_to((position >= FULL_LEN).astype(jnp.int32), (GROUPS, TOK_DEV))
    return jnp.where(whole[:, None], full_ids, split_ids).reshape(-1).astype(jnp.int32)


def block_levels(rng, shape, pieces, low, largest):
    def one(dim, blocks):
        draws = jax.random.uniform(jax.random.fold_in(jax.random.fold_in(rng, 6), dim), (blocks,), jnp.float32, low / len(pieces), largest / len(pieces))
        return jnp.repeat(jnp.exp(draws), shape[dim] // blocks).reshape((-1,) + (1,) * (len(shape) - dim - 1))

    factor_of = one(*pieces[0])
    for cut in pieces[1:]:
        factor_of = factor_of * one(*cut)
    return factor_of


def noise(key, shape, scale, bound, shards=(), kind=jnp.bfloat16):
    entries = jax.random.normal(key, shape, jnp.float32) * scale
    if len(shards) > 0:
        entries = block_levels(key, shape, shards, -0.22, 0.18) * entries
    return jnp.clip(entries, min=-bound, max=bound).astype(kind)


def setup_inputs(seed: int = 0) -> dict:
    keys = jax.random.split(jax.random.key(seed), 18)
    tokens = noise(keys[0], (TOKENS, D), 1.0, 6.0, ((0, 16), (1, 2)))
    norm1_gain = jnp.clip(1.0 + 0.1 * jax.random.normal(keys[1], (D,), jnp.float32), 0.5, 1.5)
    norm1_bias = noise(keys[2], (D,), 0.3, 1.5, (), jnp.float32)
    qkv_weight = noise(keys[3], (D, 3, D), D ** -0.5, 0.21875, ((2, 2),))
    qv_bias = noise(keys[4], (2, D), 0.5, 2.5, ((1, 2),), jnp.float32)
    out_weight = noise(keys[5], (D, D), 8 ** -0.5, 2.0, ((0, 2),))
    out_bias = noise(keys[6], (D,), 0.3, 1.5, (), jnp.float32)
    norm2_gain = jnp.clip(1.0 + 0.1 * jax.random.normal(keys[7], (D,), jnp.float32), 0.5, 1.5)
    norm2_bias = noise(keys[8], (D,), 0.3, 1.5, (), jnp.float32)
    up_weight = noise(keys[9], (D, FF), D ** -0.5, 0.21875, ((1, 2),))
    up_bias = noise(keys[10], (FF,), 0.5, 2.5, ((0, 2),), jnp.float32)
    down_weight = noise(keys[11], (FF, D), FF ** -0.5, 0.109375, ((0, 2),))
    down_bias = noise(keys[12], (D,), 0.3, 1.5, (), jnp.float32)
    out_grad = noise(keys[13], (TOKENS, D), 1.0, 6.0, ((0, 16), (1, 2)))
    send_slot = draw_send_slot(jax.random.fold_in(keys[17], 71), 0)
    pack_index = draw_pack_index(jax.random.fold_in(keys[17], 71), 0)
    clip_ids = draw_clip_ids(jax.random.fold_in(keys[17], 71), 0)
    return {"tokens": tokens, "norm1_gain": norm1_gain, "norm1_bias": norm1_bias, "qkv_weight": qkv_weight, "qv_bias": qv_bias, "out_weight": out_weight, "out_bias": out_bias, "norm2_gain": norm2_gain, "norm2_bias": norm2_bias, "up_weight": up_weight, "up_bias": up_bias, "down_weight": down_weight, "down_bias": down_bias, "out_grad": out_grad, "send_slot": send_slot, "pack_index": pack_index, "clip_ids": clip_ids}


HIGHEST = lax.Precision.HIGHEST
NORM_EPS = 1e-06
MASK_FILL = -1e+30

@jax.custom_vjp
def low(v):
    return lax.optimization_barrier(v.astype(jnp.bfloat16)).astype(jnp.float32)

@jax.custom_vjp
def low_back(v):
    return v

def low_keep(v):
    return (low(v), None)

def low_pass(kept, grad):
    return (grad,)

def back_keep(v):
    return (v, None)

def back_low(kept, grad):
    return (low(grad),)
low.defvjp(low_keep, low_pass)
low_back.defvjp(back_keep, back_low)

def round_both(values):
    return low_back(low(values))

def norm_rows(values, gain_vec, shift_vec):
    center = values - lax.optimization_barrier(jnp.mean(values, axis=-1, keepdims=True))
    spread = lax.optimization_barrier(jnp.mean(center * center, axis=-1, keepdims=True))
    return center * lax.rsqrt(spread + NORM_EPS) * gain_vec + shift_vec

def group_layer(params, group_rows, group_clip):
    gain_one, shift_one, qkv_w, qv_b, out_w, out_b, gain_two, shift_two, up_w, up_b, down_w, down_b = params
    row_count = group_rows.shape[0]
    normed = low(norm_rows(group_rows, gain_one, shift_one))
    projected = jnp.einsum('rd,dtc->rtc', normed, qkv_w, precision=HIGHEST)
    query_rows = round_both(projected[:, 0] + qv_b[0]).reshape(row_count, HEADS, HEAD_DIM)
    key_rows = round_both(projected[:, 1]).reshape(row_count, HEADS, HEAD_DIM)
    value_rows = round_both(projected[:, 2] + qv_b[1]).reshape(row_count, HEADS, HEAD_DIM)
    raw_scores = jnp.einsum('qhd,khd->hqk', query_rows, key_rows, precision=HIGHEST) * HEAD_DIM ** (-0.5)
    same_clip = group_clip[:, None] == group_clip[None, :]
    scores = jnp.where(same_clip[None], low_back(raw_scores), MASK_FILL)
    probs = low(jax.nn.softmax(scores, axis=-1))
    mixed = round_both(jnp.einsum('hqk,khd->qhd', probs, value_rows, precision=HIGHEST)).reshape(row_count, D)
    middle = group_rows + low_back(jnp.dot(mixed, out_w, precision=HIGHEST)) + out_b
    normed_two = low(norm_rows(middle, gain_two, shift_two))
    hidden_pre = low_back(jnp.dot(normed_two, up_w, precision=HIGHEST) + up_b)
    hidden = low(jax.nn.gelu(hidden_pre, approximate=False))
    return middle + jnp.dot(hidden, down_w, precision=HIGHEST) + down_b

def reference(tokens, norm1_gain, norm1_bias, qkv_weight, qv_bias, out_weight, out_bias, norm2_gain, norm2_bias, up_weight, up_bias, down_weight, down_bias, out_grad, send_slot, pack_index, clip_ids):
    slot_total = GROUPS * CAP
    source = jnp.arange(TOKENS, dtype=jnp.int32)
    arrive = send_slot // CAP * slot_total + source // TOK_DEV * CAP + send_slot % CAP
    table = jnp.zeros((GROUPS * slot_total,), jnp.int32).at[arrive].set(source)
    order = table[source // TOK_DEV * slot_total + pack_index]
    packed = tokens.astype(jnp.float32)[order].reshape(GROUPS, TOK_DEV, D)
    packed_grad = out_grad.astype(jnp.float32)[order].reshape(GROUPS, TOK_DEV, D)
    clips = clip_ids.reshape(GROUPS, TOK_DEV)
    params = tuple((weight_arg.astype(jnp.float32) for weight_arg in (norm1_gain, norm1_bias, qkv_weight, qv_bias, out_weight, out_bias, norm2_gain, norm2_bias, up_weight, up_bias, down_weight, down_bias)))

    def forward(weights, rows_all):

        def one_group(pair):
            return group_layer(weights, pair[0], pair[1])
        return lax.map(jax.checkpoint(one_group), (rows_all, clips))
    result, pull_back = jax.vjp(forward, params, packed)
    weight_grads, input_grad = pull_back(packed_grad)
    out = jnp.zeros((TOKENS, D), jnp.float32).at[order].set(result.reshape(TOKENS, D)).astype(jnp.bfloat16)
    tokens_grad = jnp.zeros((TOKENS, D), jnp.float32).at[order].set(input_grad.reshape(TOKENS, D)).astype(jnp.bfloat16)
    return (out, tokens_grad, weight_grads[0], weight_grads[1], weight_grads[2], weight_grads[3], weight_grads[4], weight_grads[5], weight_grads[6], weight_grads[7], weight_grads[8], weight_grads[9], weight_grads[10], weight_grads[11])
```

```python
import jax
import jax.numpy as jnp
from jax import lax
from jax.sharding import PartitionSpec as P

HEAD_DIM = 64
NORM_EPS = 1e-06
MASK_FILL = -1e30
BF = jnp.bfloat16
F32 = jnp.float32


def dot(a, b, dims):
    return lax.dot_general(a, b, (dims, ((), ())), preferred_element_type=F32)


def norm_stats(values):
    center = values - jnp.mean(values, axis=-1, keepdims=True)
    spread = jnp.mean(center * center, axis=-1, keepdims=True)
    scale = lax.rsqrt(spread + NORM_EPS)
    return center * scale, scale


def norm_back(grad, gain, unit, scale):
    n = grad * gain
    mean_n = jnp.mean(n, axis=-1, keepdims=True)
    mean_nx = jnp.mean(n * unit, axis=-1, keepdims=True)
    return scale * (n - mean_n - unit * mean_nx)


def gelu_pair(u):
    cdf = 0.5 * (1.0 + lax.erf(u * (0.5**0.5)))
    return u * cdf, cdf + u * jnp.exp(-0.5 * u * u) * 0.3989422804014327


def halves(array, index, axis):
    size = array.shape[axis] // 2
    mine = lax.dynamic_slice_in_dim(array, index * size, size, axis)
    other = lax.dynamic_slice_in_dim(array, (1 - index) * size, size, axis)
    return mine, other


def join(mine, other, index, axis):
    first = index == 0
    return jnp.concatenate(
        [jnp.where(first, mine, other), jnp.where(first, other, mine)], axis=axis
    )


def exchange(array, axis_name, bit, size):
    return lax.ppermute(array, axis_name, [(i, i ^ bit) for i in range(size)])


def swap(array):
    return exchange(array, "mp", 1, 2)


def reduce_rows(array, order, dp_index, dp_size):
    rows, columns = array.shape
    bits = dp_size.bit_length() - 1
    view = array.reshape((2,) * bits + (rows // dp_size, columns))
    left = list(range(bits - 1, -1, -1))
    for place, bit in enumerate(order):
        axis = left.index(bit)
        mine = (dp_index >> bit) & 1
        keep = lax.dynamic_index_in_dim(view, mine, axis, keepdims=False)
        send = lax.dynamic_index_in_dim(view, 1 - mine, axis, keepdims=False)
        got = exchange(send, "dp", 1 << bit, dp_size)
        view = keep.astype(F32) + got.astype(F32)
        if place < bits - 1:
            view = view.astype(BF)
        left.remove(bit)
    return view


def masked_scores(query_block, key_rows, clip_block, clip_all, score_scale):
    raw_scores = (
        jnp.einsum("qhd,khd->hqk", query_block, key_rows, preferred_element_type=F32) * score_scale
    )
    same_clip = clip_block[:, None] == clip_all[None, :]
    return jnp.where(same_clip[None], raw_scores, MASK_FILL)


def attend_forward(query, key, value, clip_ids):
    row_count, half_width = query.shape
    heads = half_width // HEAD_DIM
    query_rows, key_rows, value_rows = (
        a.reshape(row_count, heads, HEAD_DIM) for a in (query, key, value)
    )
    score_scale = HEAD_DIM ** (-0.5)
    block_rows = min(512, row_count)

    def attend(block_index):
        start = block_index * block_rows
        query_block = lax.dynamic_slice_in_dim(query_rows, start, block_rows, 0)
        clip_block = lax.dynamic_slice_in_dim(clip_ids, start, block_rows, 0)
        scores = masked_scores(query_block, key_rows, clip_block, clip_ids, score_scale)
        row_max = jnp.max(scores, axis=-1, keepdims=True)
        exponent = jnp.exp(scores - row_max)
        row_total = jnp.sum(exponent, axis=-1, keepdims=True)
        probs_low = (exponent / row_total).astype(BF)
        mixed = jnp.einsum("hqk,khd->qhd", probs_low, value_rows, preferred_element_type=F32)
        return mixed.astype(BF), (row_max + jnp.log(row_total))[..., 0]

    mixed, log_totals = lax.map(attend, jnp.arange(row_count // block_rows))
    return mixed.reshape(row_count, half_width), log_totals


def attend_backward(query, key, value, clip_ids, log_totals, mixed, mixed_grad):
    row_count, half_width = query.shape
    heads = half_width // HEAD_DIM
    query_rows, key_rows, value_rows, mixed_grad = (
        a.reshape(row_count, heads, HEAD_DIM) for a in (query, key, value, mixed_grad)
    )
    score_scale = HEAD_DIM ** (-0.5)
    block_rows = min(512, row_count)

    def back(carried, block_index):
        key_acc, value_acc = carried
        start = block_index * block_rows
        query_block = lax.dynamic_slice_in_dim(query_rows, start, block_rows, 0)
        clip_block = lax.dynamic_slice_in_dim(clip_ids, start, block_rows, 0)
        grad_block = lax.dynamic_slice_in_dim(mixed_grad, start, block_rows, 0)
        scores = masked_scores(query_block, key_rows, clip_block, clip_ids, score_scale)
        probs = jnp.exp(scores - log_totals[block_index][..., None])
        probs_low = probs.astype(BF)
        prob_grad = jnp.einsum("qhd,khd->hqk", grad_block, value_rows, preferred_element_type=F32)
        inner_sum = jnp.sum(prob_grad * probs, axis=-1, keepdims=True)
        score_grad = (probs * (prob_grad - inner_sum)).astype(BF)
        query_grad = (
            jnp.einsum("hqk,khd->qhd", score_grad, key_rows, preferred_element_type=F32)
            * score_scale
        )
        key_acc = (
            key_acc
            + jnp.einsum("hqk,qhd->khd", score_grad, query_block, preferred_element_type=F32)
            * score_scale
        )
        value_acc = value_acc + jnp.einsum(
            "hqk,qhd->khd", probs_low, grad_block, preferred_element_type=F32
        )
        return (key_acc, value_acc), query_grad.astype(BF)

    zero = jnp.zeros((row_count, heads, HEAD_DIM), F32)
    (key_total, value_total), query_blocks = lax.scan(
        back, (zero, zero), jnp.arange(row_count // block_rows)
    )
    parts = (query_blocks, key_total.astype(BF), value_total.astype(BF))
    return jnp.concatenate([p.reshape(row_count, half_width) for p in parts], axis=1)


def to_groups(rows, send_slot, dp_size):
    slots = jnp.zeros((2 * rows.shape[0], rows.shape[1]), BF).at[send_slot].set(rows)
    return lax.all_to_all(slots, "dp", split_axis=0, concat_axis=0, tiled=True)


def to_entry(rows, pack_index, send_slot):
    slots = jnp.zeros((2 * rows.shape[0], rows.shape[1]), BF).at[pack_index].set(rows)
    back = lax.all_to_all(slots, "dp", split_axis=0, concat_axis=0, tiled=True)
    return back[send_slot]


def local(dp_size, *args):
    (
        tokens,
        norm1_gain,
        norm1_bias,
        qkv_weight,
        qv_bias,
        out_weight,
        out_bias,
        norm2_gain,
        norm2_bias,
        up_weight,
        up_bias,
        down_weight,
        down_bias,
        out_grad,
        send_slot,
        pack_index,
        clip_ids,
    ) = args
    row_count, half = tokens.shape
    width = 2 * half
    m = lax.axis_index("mp")
    dp_index = lax.axis_index("dp")
    bits = dp_size.bit_length() - 1
    low_first = list(range(bits))
    swap_first = [1, 0] + low_first[2:]

    out_w_o, up_w_o, down_w_o = swap(out_weight), swap(up_weight), swap(down_weight)
    up_b_o = swap(up_bias)
    qkv_flat = qkv_weight.reshape(width, 3 * half)
    zero_half = jnp.zeros((half,), F32)
    proj_bias = jnp.concatenate([qv_bias[0], zero_half, qv_bias[1]])

    recv_rows = to_groups(tokens, send_slot, dp_size)
    recv_rows, grads_in = lax.optimization_barrier((recv_rows, out_grad))
    recv_grads = to_groups(grads_in, send_slot, dp_size)

    my_index, other_index = halves(pack_index, m, 0)
    turned_index = jnp.concatenate([my_index, other_index])

    x_half = recv_rows[pack_index]
    x_low = join(x_half, swap(x_half), m, 1)
    x = x_low.astype(F32)
    unit1, _ = norm_stats(x)
    h1 = (unit1 * norm1_gain + norm1_bias).astype(BF)
    proj = (dot(h1, qkv_flat, ((1,), (0,))) + proj_bias).astype(BF)
    query, key, value = proj[:, :half], proj[:, half : 2 * half], proj[:, 2 * half :]
    mixed, log_totals = attend_forward(query, key, value, clip_ids)

    mixed_my, mixed_send = halves(mixed, m, 0)
    mixed_o = swap(mixed_send)
    x_my = halves(x_low, m, 0)[0].astype(F32)
    x2 = (
        x_my
        + (dot(mixed_my, out_weight, ((1,), (0,))) + dot(mixed_o, out_w_o, ((1,), (0,))))
        + out_bias
    )
    unit2, scale2 = norm_stats(x2)
    h2 = (unit2 * norm2_gain + norm2_bias).astype(BF)
    g_m, gp_m = gelu_pair(dot(h2, up_weight, ((1,), (0,))) + up_bias)
    g_o, gp_o = gelu_pair(dot(h2, up_w_o, ((1,), (0,))) + up_b_o)
    g_m, g_o, gp_m, gp_o = (a.astype(BF) for a in (g_m, g_o, gp_m, gp_o))
    y = (
        x2 + (dot(g_m, down_weight, ((1,), (0,))) + dot(g_o, down_w_o, ((1,), (0,)))) + down_bias
    ).astype(BF)

    grad_half = recv_grads[turned_index]
    half_rows = row_count // 2
    dy_low = join(grad_half[:half_rows], swap(grad_half[half_rows:]), m, 1)
    dy = dy_low.astype(F32)
    du_m = (dot(dy_low, down_weight, ((1,), (1,))) * gp_m.astype(F32)).astype(BF)
    du_o = (dot(dy_low, down_w_o, ((1,), (1,))) * gp_o.astype(F32)).astype(BF)
    dh2 = dot(du_m, up_weight, ((1,), (1,))) + dot(du_o, up_w_o, ((1,), (1,)))
    dx2 = dy + norm_back(dh2, norm2_gain, unit2, scale2)
    da = dx2.astype(BF)
    do_m = dot(da, out_weight, ((1,), (1,))).astype(BF)
    do_o = dot(da, out_w_o, ((1,), (1,))).astype(BF)
    do = join(do_m, swap(do_o), m, 0)

    y_my, y_send = halves(y, m, 1)
    out = to_entry(jnp.concatenate([y_my, swap(y_send)]), turned_index, send_slot)

    first = lambda a, b: dot(a, b, ((0,), (0,)))
    up_grad_o = swap(first(h2, du_o).astype(BF))
    down_grad_o = swap(first(dy_low, g_o).astype(BF))
    out_grad_o = swap(first(da, mixed_o).astype(BF))
    up_grad = (first(h2, du_m) + up_grad_o.astype(F32)).astype(BF)
    down_grad = (first(dy_low, g_m) + down_grad_o.astype(F32)).astype(BF)
    out_w_grad = (first(da, mixed_my) + out_grad_o.astype(F32)).astype(BF)
    up_grad = reduce_rows(up_grad, low_first, dp_index, dp_size)
    down_grad = reduce_rows(down_grad, swap_first, dp_index, dp_size)
    out_w_grad = reduce_rows(out_w_grad, swap_first, dp_index, dp_size)

    d_proj = attend_backward(query, key, value, clip_ids, log_totals, mixed, do)

    dp_my, dp_send = halves(d_proj, m, 0)
    dh1_send = dot(dp_send, qkv_flat, ((1,), (1,))).astype(BF)
    dh1 = dot(dp_my, qkv_flat, ((1,), (1,))) + swap(dh1_send).astype(F32)
    unit1_my, scale1_my = norm_stats(x_my)
    dx = (dx2 + norm_back(dh1, norm1_gain, unit1_my, scale1_my)).astype(BF)
    dx_my, dx_send = halves(dx, m, 1)
    tokens_grad = to_entry(jnp.concatenate([dx_my, swap(dx_send)]), turned_index, send_slot)

    qkv_grad = first(h1, d_proj).astype(BF)
    qkv_grad = reduce_rows(qkv_grad, low_first, dp_index, dp_size)

    total = lambda a: jnp.sum(a.astype(F32), axis=0)
    shared = [
        total(dh1 * unit1_my),
        total(dh1),
        total(dx2),
        total(dh2 * unit2),
        total(dh2),
        total(dy),
    ]
    both = jnp.concatenate(shared + [total(du_m)])
    both = both + swap(jnp.concatenate(shared + [total(du_o)]))
    small = jnp.concatenate([both, total(d_proj)])
    for bit in range(bits):
        small = small + exchange(small, "dp", 1 << bit, dp_size)
    n1g, n1b, ob, n2g, n2b, db = (small[i * width : (i + 1) * width] for i in range(6))
    rest = small[6 * width :]
    hidden = up_bias.shape[0]
    up_b_grad, proj_b_grad = rest[:hidden], rest[hidden:]
    qv_grad = jnp.stack([proj_b_grad[:half], proj_b_grad[2 * half :]])

    return (
        out,
        tokens_grad,
        n1g,
        n1b,
        qkv_grad.reshape(-1, 3, half),
        qv_grad,
        out_w_grad.T,
        ob,
        n2g,
        n2b,
        up_grad,
        up_b_grad,
        down_grad.T,
        db,
    )


def solution(mesh):
    dp_size = mesh.shape["dp"]
    in_specs = (
        P("dp", "mp"),
        P(),
        P(),
        P(None, None, "mp"),
        P(None, "mp"),
        P("mp", None),
        P(),
        P(),
        P(),
        P(None, "mp"),
        P("mp"),
        P("mp", None),
        P(),
        P("dp", "mp"),
        P("dp"),
        P("dp"),
        P("dp"),
    )
    out_specs = (
        P("dp", "mp"),
        P("dp", "mp"),
        P(),
        P(),
        P("dp", None, "mp"),
        P(None, "mp"),
        P("mp", "dp"),
        P(),
        P(),
        P(),
        P("dp", "mp"),
        P("mp"),
        P("mp", "dp"),
        P(),
    )

    def run(*args):
        return local(dp_size, *args)

    return jax.shard_map(run, mesh=mesh, in_specs=in_specs, out_specs=out_specs, check_vma=False)
```
